32 devices in a mesh: band: 4 (over y, core), fft: 8 (over z, x).
Axes of the slice: x: 2, y: 2, z: 4, core: 2. Of those that a mesh axis runs over, the one named last changes fastest.
Arguments:
- start_bands: float32 [2, 8, 96, 9216], P(None, 'band', 'fft'), may hold values from -6 to 6
- potential: float32 [96, 96, 96], P(None, None, 'fft'), may hold values from -2 to 1
- half_height: int32 [96, 96], P('fft'), may hold values from -1 to 24, as said below
- lower_bound: float32 [1], replicated, may hold values from 1 to 2
- upper_bound: float32 [1], replicated, may hold values from 14 to 16
- fermi_level: float32 [1], replicated, may hold values from 0 to 2
Outputs:
- filtered_bands: float32 [2, 8, 96, 9216], P(None, 'band', 'fft')
- energies: float32 [8], P('band')
- band_energy: float32 [1], replicated
The draws below stay inside these ranges and needn't reach their ends.
Inputs may be any that keep to these rules, and one draw needn't show every extreme that they name: Column (x, y) keeps exactly the wave vectors whose z frequency f has |f| <= half_height[x, y]; -1 marks an empty column; the column of x = y = 0 holds 24; every column whose x or y frequency exceeds 96/4 in magnitude is empty.
All inputs are finite; a program needn't handle non-finite values.
Results may differ from the reference program's by a relative error of at most 0.0003.
Values sent between devices are 32-bit elements; how exact they have to be, the bound alone decides.
No kernel may reach another device: no remote copies, remote signals or barrier semaphores. Data moves between devices by JAX's collectives and lax.ppermute only.
A program may use at most 128 MiB of HBM per device.

```python
import jax
import jax.numpy as jnp
from jax import lax

NG = 96
DEGREE = 3
BANDS = 8
CELLS = 884736


def draw_half_height(key, part):
    quarter = NG // 4
    radius_sq = quarter * quarter + jax.random.randint(key, (), 0, quarter, dtype=jnp.int32)
    positions = jnp.arange(NG, dtype=jnp.int32)
    frequency = jnp.where(positions < NG // 2, positions, positions - NG)
    remaining = radius_sq - frequency[:, None] ** 2 - frequency[None, :] ** 2
    z_values = jnp.arange(NG // 2, dtype=jnp.int32)
    z_count = jnp.sum((z_values[None, None, :] ** 2 <= remaining[:, :, None]).astype(jnp.int32), axis=2)
    return z_count - 1


def shard_levels(key, extent, shards, smallest, largest):
    def one(position, parts):
        heights = jax.random.uniform(jax.random.fold_in(jax.random.fold_in(key, 6), position), (parts,), jnp.float32, smallest / len(shards), largest / len(shards))
        return jnp.repeat(jnp.exp(heights), extent[position] // parts).reshape((-1,) + (1,) * (len(extent) - position - 1))

    level = one(*shards[0])
    for cut in shards[1:]:
        level = level * one(*cut)
    return level


def scatter_about(key, extent, spread, most, split=(), held_as=jnp.bfloat16):
    gain = shard_levels(key, extent, split, -0.22, 0.18) if split else 1.0
    result = jax.random.normal(key, extent, jnp.float32) * spread * gain
    return jnp.minimum(jnp.maximum(result, -most), most).astype(held_as)


def setup_inputs(seed: int = 0) -> dict:
    key_list = jax.random.split(jax.random.key(seed), 7)
    return {
        "start_bands": scatter_about(key_list[0], (2, BANDS, NG, NG * NG), 1.0, 6.0, ((1, 4), (2, 8)), jnp.float32),
        "potential": jnp.clip(-2.0 + 3.0 * jax.random.uniform(key_list[1], (NG, NG, NG), jnp.float32) ** shard_levels(key_list[1], (NG, NG, NG), ((2, 8),), -0.2, 0.2), -2.0, 1.0),
        "half_height": draw_half_height(jax.random.fold_in(key_list[6], 71), 0),
        "lower_bound": jnp.clip(jax.random.uniform(key_list[3], (1,), jnp.float32, 1.0, 2.0), 1.0, 2.0),
        "upper_bound": jnp.clip(jax.random.uniform(key_list[4], (1,), jnp.float32, 14.0, 16.0), 14.0, 16.0),
        "fermi_level": jnp.clip(jax.random.uniform(key_list[5], (1,), jnp.float32, 0.0, 2.0), 0.0, 2.0),
    }


KIN_MAX = 12.0
TEMPER = 0.5
HIGHEST = lax.Precision.HIGHEST

def frequency_of(length):
    positions = jnp.arange(length, dtype=jnp.int32)
    return jnp.where(positions < length // 2, positions, positions - length)

def sphere_tables(half_height):
    frequency = frequency_of(NG)
    inside = (jnp.abs(frequency)[None, None, :] <= half_height[:, :, None]).astype(jnp.float32)
    squared = frequency[:, None, None] ** 2 + frequency[None, :, None] ** 2 + frequency[None, None, :] ** 2
    kinetic = KIN_MAX / (NG // 4) ** 2 * squared.astype(jnp.float32)
    return (inside, kinetic)

def hamiltonian(field, potential, inside, kinetic):

    def one_band(pair_parts):
        real_part, imag_part = pair_parts
        space = jnp.fft.ifftn(lax.complex(real_part, imag_part)) * potential
        back = jnp.fft.fftn(space)
        return (inside * (kinetic * real_part + jnp.real(back)), inside * (kinetic * imag_part + jnp.imag(back)))
    real_out, imag_out = lax.map(one_band, (field[0], field[1]))
    return jnp.stack([real_out, imag_out])

def reference(start_bands, potential, half_height, lower_bound, upper_bound, fermi_level):
    shaped = start_bands.reshape(2, BANDS, NG, NG, NG)
    inside, kinetic = sphere_tables(half_height)
    center = 0.5 * (upper_bound[0] + lower_bound[0])
    half_width = 0.5 * (upper_bound[0] - lower_bound[0])
    previous = inside * shaped
    current = (hamiltonian(previous, potential, inside, kinetic) - center * previous) / half_width
    for degree_step in range(1, DEGREE):
        following = 2.0 * (hamiltonian(current, potential, inside, kinetic) - center * current) / half_width - previous
        previous, current = (current, following)
    real_rows = current[0].reshape(BANDS, CELLS)
    imag_rows = current[1].reshape(BANDS, CELLS)
    gram_real = (jnp.dot(real_rows, real_rows.T, precision=HIGHEST) + jnp.dot(imag_rows, imag_rows.T, precision=HIGHEST)) / CELLS
    gram_imag = (jnp.dot(real_rows, imag_rows.T, precision=HIGHEST) - jnp.dot(imag_rows, real_rows.T, precision=HIGHEST)) / CELLS
    embedded = jnp.block([[gram_real, -gram_imag], [gram_imag, gram_real]])
    factor = jnp.linalg.cholesky(embedded)
    selector = jnp.eye(2 * BANDS, BANDS, dtype=jnp.float32)
    inverse_cols = lax.linalg.triangular_solve(factor, selector, left_side=True, lower=True, transpose_a=True)
    upper_rows = inverse_cols[:BANDS]
    lower_rows = inverse_cols[BANDS:]
    rot_real = jnp.dot(upper_rows.T, real_rows, precision=HIGHEST) - jnp.dot(lower_rows.T, imag_rows, precision=HIGHEST)
    rot_imag = jnp.dot(upper_rows.T, imag_rows, precision=HIGHEST) + jnp.dot(lower_rows.T, real_rows, precision=HIGHEST)
    rotated = jnp.stack([rot_real, rot_imag]).reshape(2, BANDS, NG, NG, NG)
    applied = hamiltonian(rotated, potential, inside, kinetic)
    energies = jnp.sum((rotated * applied).reshape(2, BANDS, CELLS), axis=(0, 2)) / CELLS
    weights = jax.nn.sigmoid((fermi_level[0] - energies) / TEMPER)
    band_energy = (jnp.sum(weights * energies) / BANDS).reshape(1)
    return (rotated.reshape(2, BANDS, NG, NG * NG), energies, band_energy)
```

```python
import functools
import math

import jax
import jax.numpy as jnp
import numpy as np
from jax import lax
from jax.experimental import pallas as pl
from jax.experimental.pallas import tpu as pltpu
from jax.sharding import Mesh
from jax.sharding import PartitionSpec as P

DEGREE = 3
KIN_MAX = 12.0
TEMPER = 0.5
XP = 64
BF = jnp.bfloat16
F32 = jnp.float32
AXES = ("bh", "bl", "fh", "fl")
BAND = ("bh", "bl")
FFT = ("fh", "fl")
GROUP = ("bl", "fl")
PEERS = ("bh", "fh")


def round_up(value, unit):
    return -(-value // unit) * unit


class Plan:
    def __init__(self, length, group, peers, bands, band_block):
        quarter = length // 4
        self.length = length
        self.quarter = quarter
        self.kept = 2 * quarter + 1
        self.group = group
        self.peers = peers
        self.bands = bands
        self.band_block = band_block
        self.ky = -(-self.kept // group)
        self.ky_all = self.ky * group
        self.zl = length // group
        self.zrow = round_up(2 * self.zl, 8)
        self.fz = round_up(self.kept, 8)
        self.rows = 2 * self.fz
        self.lanes = band_block * XP
        self.wide = round_up(length, 128)
        self.freq = np.concatenate([np.arange(quarter + 1), np.arange(-quarter, 0)])


def phase(freq, pos, length):
    angle = 2.0 * np.pi / length * ((freq[:, None] * pos[None, :]) % length)
    return np.cos(angle), np.sin(angle)


def split_np(table):
    high = np.asarray(table, np.float32).astype(BF)
    low = np.asarray(table - high.astype(np.float64), np.float32).astype(BF)
    return high, low


def left_table(table):
    high, low = split_np(table)
    return np.concatenate([high, high, low], axis=1)


def right_table(table):
    high, low = split_np(table)
    return np.concatenate([high, high, low], axis=0)


def build_tables(p):
    cos, sin = phase(p.freq, np.arange(p.length), p.length)
    kept, length = p.kept, p.length
    to_z = np.zeros((p.group, p.zrow, 2, p.fz))
    for m in range(p.group):
        here = slice(m * p.zl, (m + 1) * p.zl)
        to_z[m, : p.zl, 0, :kept] = cos[:, here].T
        to_z[m, : p.zl, 1, :kept] = -sin[:, here].T
        to_z[m, p.zl : 2 * p.zl, 0, :kept] = sin[:, here].T
        to_z[m, p.zl : 2 * p.zl, 1, :kept] = cos[:, here].T
    to_z = to_z.reshape(p.group * p.zrow, p.rows)
    from_z = np.ascontiguousarray(to_z.T)
    to_y = np.zeros((2, length, 2, p.ky_all))
    to_y[0, :, 0, :kept] = cos.T
    to_y[0, :, 1, :kept] = -sin.T
    to_y[1, :, 0, :kept] = sin.T
    to_y[1, :, 1, :kept] = cos.T
    to_y = to_y.reshape(2 * length, 2 * p.ky_all)
    from_y = np.ascontiguousarray(to_y.T)
    to_x = np.zeros((2, p.band_block, XP, p.band_block, 2, p.wide))
    for b in range(p.band_block):
        to_x[0, b, :kept, b, 0, :length] = cos
        to_x[0, b, :kept, b, 1, :length] = sin
        to_x[1, b, :kept, b, 0, :length] = -sin
        to_x[1, b, :kept, b, 1, :length] = cos
    to_x = to_x.reshape(2 * p.lanes, p.band_block * 2 * p.wide)
    from_x = np.ascontiguousarray(to_x.T)
    return {
        "to_z": left_table(to_z),
        "from_z": left_table(from_z),
        "to_y": left_table(to_y),
        "from_y": left_table(from_y),
        "to_x": right_table(to_x),
        "from_x": right_table(from_x),
    }


def split(value):
    high = value.astype(BF)
    low = (value - high.astype(F32)).astype(BF)
    return high, low


def left_mul(table, value):
    high, low = split(value)
    stacked = jnp.concatenate([high, low, high], axis=0)
    return jnp.dot(table, stacked, preferred_element_type=F32)


def right_mul(value, table):
    high, low = split(value)
    stacked = jnp.concatenate([high, low, high], axis=1)
    return jnp.dot(stacked, table, preferred_element_type=F32)


def z_kernel(p, has_back, has_prev, has_field, has_fwd, has_energy, *refs):
    refs = list(refs)
    scal = refs.pop(0)
    cols = refs.pop(0)
    field = refs.pop(0)
    back = refs.pop(0) if has_back else None
    prev = refs.pop(0) if has_prev else None
    from_z = refs.pop(0) if has_back else None
    to_z = refs.pop(0) if has_fwd else None
    out_field = refs.pop(0) if has_field else None
    out_fwd = refs.pop(0) if has_fwd else None
    out_energy = refs.pop(0) if has_energy else None
    index = lax.broadcasted_iota(jnp.int32, (p.fz, p.lanes), 0)
    freq = jnp.where(index <= p.quarter, index, index - p.kept)
    height = cols[0, 0:1, :]
    inside = jnp.where(
        (jnp.abs(freq).astype(F32) <= height) & (index < p.kept), 1.0, 0.0
    ).astype(F32)
    inside = jnp.concatenate([inside, inside], axis=0)
    squared = cols[0, 1:2, :] + (freq * freq).astype(F32)
    kinetic = KIN_MAX / p.quarter**2 * squared
    kinetic = jnp.concatenate([kinetic, kinetic], axis=0)
    value = field[0]
    if has_back:
        spread = back[...].reshape(p.group * p.zrow, p.lanes)
        moved = left_mul(from_z[...], spread)
        applied = inside * (kinetic * value + (1.0 / p.length**3) * moved)
        value = scal[0] * (applied - scal[1] * value)
        if has_prev:
            value = 2.0 * value - prev[0]
    else:
        value = jnp.where(inside > 0.0, value, 0.0)
    if has_field:
        out_field[0] = value
    if has_energy:
        out_energy[0] = (kinetic * value * value).reshape(-1, 8, p.lanes).sum(axis=0)
    if has_fwd:
        out_fwd[...] = left_mul(to_z[...], value).reshape(p.group, 1, p.zrow, p.lanes)


def z_stage(p, tables, scal, cols, field, back=None, prev=None, fwd=True, energy=False):
    has_field = not energy
    plane = pl.BlockSpec((1, p.rows, p.lanes), lambda i: (i, 0, 0))
    chunk = pl.BlockSpec((p.group, 1, p.zrow, p.lanes), lambda i: (0, i, 0, 0))
    whole = lambda a: pl.BlockSpec(a.shape, lambda i: (0,) * a.ndim)
    args = [scal, cols, field]
    specs = [
        pl.BlockSpec(memory_space=pltpu.SMEM),
        pl.BlockSpec((1, 8, p.lanes), lambda i: (i, 0, 0)),
        plane,
    ]
    if back is not None:
        args.append(back)
        specs.append(chunk)
    if prev is not None:
        args.append(prev)
        specs.append(plane)
    if back is not None:
        table = jnp.asarray(tables["from_z"])
        args.append(table)
        specs.append(whole(table))
    if fwd:
        table = jnp.asarray(tables["to_z"])
        args.append(table)
        specs.append(whole(table))
    outs, out_specs = [], []
    if has_field:
        outs.append(jax.ShapeDtypeStruct((p.ky, p.rows, p.lanes), F32))
        out_specs.append(plane)
    if fwd:
        outs.append(jax.ShapeDtypeStruct((p.group, p.ky, p.zrow, p.lanes), F32))
        out_specs.append(chunk)
    if energy:
        outs.append(jax.ShapeDtypeStruct((p.ky, 8, p.lanes), F32))
        out_specs.append(pl.BlockSpec((1, 8, p.lanes), lambda i: (i, 0, 0)))
    body = functools.partial(
        z_kernel, p, back is not None, prev is not None, has_field, fwd, energy
    )
    return pl.pallas_call(
        body, grid=(p.ky,), in_specs=specs, out_specs=out_specs, out_shape=outs, name="z_stage"
    )(*args)


def mid_kernel(p, block, energy, data, potential, to_y, to_x, *rest):
    if energy:
        (out,) = rest
    else:
        from_x, from_y, out = rest
    length = p.length
    total = [0.0] * p.band_block
    for start in range(0, p.zl, block):
        rows = []
        for z in range(start, start + block):
            real = data[pl.ds(z, p.ky_all, stride=p.zrow), :]
            imag = data[pl.ds(p.zl + z, p.ky_all, stride=p.zrow), :]
            rows.append(jnp.concatenate([real, imag], axis=0))
        lined = left_mul(to_y[...], jnp.concatenate(rows, axis=1))
        pieces = []
        for j in range(block):
            here = lined[:, j * p.lanes : (j + 1) * p.lanes]
            pieces.append(jnp.concatenate([here[:length], here[length:]], axis=1))
        space = right_mul(jnp.concatenate(pieces, axis=0), to_x[...])
        local = potential[start : start + block].reshape(block * length, p.wide)
        if energy:
            for b in range(p.band_block):
                real = space[:, 2 * b * p.wide : (2 * b + 1) * p.wide]
                imag = space[:, (2 * b + 1) * p.wide : (2 * b + 2) * p.wide]
                dens = local * (real * real + imag * imag)
                total[b] = total[b] + dens.reshape(-1, 8, p.wide).sum(axis=0)
            continue
        space = space * jnp.concatenate([local] * (2 * p.band_block), axis=1)
        ready = right_mul(space, from_x[...])
        columns = []
        for j in range(block):
            here = ready[j * length : (j + 1) * length]
            columns.append(jnp.concatenate([here[:, : p.lanes], here[:, p.lanes :]], axis=0))
        final = left_mul(from_y[...], jnp.concatenate(columns, axis=1))
        for j in range(block):
            z = start + j
            here = final[:, j * p.lanes : (j + 1) * p.lanes]
            out[pl.ds(z, p.ky_all, stride=p.zrow), :] = here[: p.ky_all]
            out[pl.ds(p.zl + z, p.ky_all, stride=p.zrow), :] = here[p.ky_all :]
    if energy:
        for b in range(p.band_block):
            out[b] = total[b]
    else:
        for spare in range(2 * p.zl, p.zrow):
            out[pl.ds(spare, p.ky_all, stride=p.zrow), :] = jnp.zeros((p.ky_all, p.lanes), F32)


def mid_stage(p, tables, data, potential, energy=False):
    block = max(d for d in range(1, 5) if p.zl % d == 0)
    rows = p.ky_all * p.zrow
    args = [data.reshape(rows, p.lanes), potential]
    names = ["to_y", "to_x"] + ([] if energy else ["from_x", "from_y"])
    args += [jnp.asarray(tables[n]) for n in names]
    shape = (p.band_block, 8, p.wide) if energy else (rows, p.lanes)
    vmem = pl.BlockSpec(memory_space=pltpu.VMEM)
    out = pl.pallas_call(
        functools.partial(mid_kernel, p, block, energy),
        in_specs=[vmem] * len(args),
        out_specs=vmem,
        out_shape=jax.ShapeDtypeStruct(shape, F32),
        name="mid_stage",
    )(*args)
    return out if energy else out.reshape(p.group, p.ky, p.zrow, p.lanes)


def exchange(value, axes):
    return lax.all_to_all(value, axes, 0, 0, tiled=True)


def collect(value, axes, count):
    return exchange(jnp.broadcast_to(value[None], (count,) + value.shape), axes)


def swap_pairs(sizes):
    bh, bl, fh, fl = sizes
    number = lambda a, b, c, d: ((a * bl + b) * fh + c) * fl + d
    return [
        (number(a, b, c, d), number(a, c, b, d))
        for a in range(bh)
        for b in range(bl)
        for c in range(fh)
        for d in range(fl)
    ]


def pick(array, axis, p):
    lower = lax.slice_in_dim(array, 0, p.quarter + 1, axis=axis)
    upper = lax.slice_in_dim(array, p.length - p.quarter, p.length, axis=axis)
    return jnp.concatenate([lower, upper], axis=axis)


def place(array, axis, p):
    lower = lax.slice_in_dim(array, 0, p.quarter + 1, axis=axis)
    upper = lax.slice_in_dim(array, p.quarter + 1, p.kept, axis=axis)
    shape = list(array.shape)
    shape[axis] = p.length - p.kept
    return jnp.concatenate([lower, jnp.zeros(tuple(shape), array.dtype), upper], axis=axis)


def pad_axis(array, axis, size, fill=0.0):
    widths = [(0, 0)] * array.ndim
    widths[axis] = (0, size - array.shape[axis])
    return jnp.pad(array, widths, constant_values=fill)


def chol_kernel(order, keep, matrix, out):
    size = matrix.shape[0]
    rows = lax.broadcasted_iota(jnp.int32, (size, 128), 0)
    lanes = lax.broadcasted_iota(jnp.int32, (size, 128), 1)
    work = matrix[...] + jnp.where(lanes == rows + order, 1.0, 0.0)
    for k in range(order):
        pivot = work[k : k + 1, k : k + 1]
        scale = 1.0 / jnp.sqrt(pivot)
        row = work[k : k + 1, :] * scale
        column = work[:, k : k + 1] * scale
        work = jnp.where(rows == k, row, work - jnp.where(rows > k, column * row, 0.0))
    out[...] = work


def inverse_factor(gram_real, gram_imag):
    bands = gram_real.shape[0]
    order = 2 * bands
    embedded = jnp.block([[gram_real, -gram_imag], [gram_imag, gram_real]])
    padded = jnp.pad(embedded, ((0, round_up(order, 8) - order), (0, 128 - order)))
    vmem = pl.BlockSpec(memory_space=pltpu.VMEM)
    out = pl.pallas_call(
        functools.partial(chol_kernel, order, bands),
        in_specs=[vmem],
        out_specs=vmem,
        out_shape=jax.ShapeDtypeStruct(padded.shape, F32),
        name="factor",
    )(padded)
    inverse = out[:bands, order : 2 * order]
    return inverse.T[:bands], inverse.T[bands:]


def gram_kernel(count, lanes, data, out):
    parts = [data[i] for i in range(2 * count)]
    swapped = [pltpu.roll(v, XP, 1) for v in parts]
    n = 0
    for i in range(2 * count):
        for j in range(2 * count):
            out[n : n + 1, :] = jnp.sum(parts[i] * parts[j], axis=0, keepdims=True)
            out[n + 1 : n + 2, :] = jnp.sum(parts[i] * swapped[j], axis=0, keepdims=True)
            n += 2


def gram_parts(p, data):
    count = p.peers
    vmem = pl.BlockSpec(memory_space=pltpu.VMEM)
    flat = data.reshape((2 * count,) + data.shape[2:])
    n = 2 * (2 * count) ** 2
    out = pl.pallas_call(
        functools.partial(gram_kernel, count, p.lanes),
        in_specs=[vmem],
        out_specs=vmem,
        out_shape=jax.ShapeDtypeStruct((n, p.lanes), F32),
        name="gram",
    )(flat)
    return out.reshape(n, p.band_block, XP).sum(axis=2)


def gram_matrices(p, sums):
    c = p.peers
    sums = sums.reshape(c, 2, c, 2, 2, 2) / float(p.length**3)
    plain = sums[..., 0, :]
    cross = sums[..., 1, :]
    eye = jnp.eye(2, dtype=F32)
    full = plain[..., :, None] * eye + cross[..., :, None] * (1.0 - eye)
    full = full.transpose(1, 3, 0, 4, 2, 5).reshape(2, 2, 2 * c, 2 * c)
    return full[0, 0] + full[1, 1], full[0, 1] - full[1, 0]


def rotate_kernel(count, data, coef, out):
    parts = [data[i] for i in range(2 * count)]
    swapped = [pltpu.roll(v, XP, 1) for v in parts]
    for t in range(2 * count):
        acc = None
        for i in range(2 * count):
            term = parts[i] * coef[t, 2 * i : 2 * i + 1, :]
            term = term + swapped[i] * coef[t, 2 * i + 1 : 2 * i + 2, :]
            acc = term if acc is None else acc + term
        out[t] = acc


def rotate(p, data, upper, lower):
    c = p.peers
    weight = jnp.stack(
        [jnp.stack([upper, lower]), jnp.stack([-lower, upper])]
    )
    weight = weight.reshape(2, 2, c, 2, c, 2)
    plain = jnp.stack([weight[:, :, :, 0, :, 0], weight[:, :, :, 1, :, 1]], axis=-1)
    cross = jnp.stack([weight[:, :, :, 1, :, 0], weight[:, :, :, 0, :, 1]], axis=-1)
    coef = jnp.stack([plain, cross], axis=-2)
    coef = coef.transpose(3, 1, 2, 0, 4, 5).reshape(2 * c, 4 * c, 2)
    coef = jnp.repeat(coef, XP, axis=-1)
    vmem = pl.BlockSpec(memory_space=pltpu.VMEM)
    flat = data.reshape((2 * c,) + data.shape[2:])
    out = pl.pallas_call(
        functools.partial(rotate_kernel, c),
        in_specs=[vmem, vmem],
        out_specs=vmem,
        out_shape=jax.ShapeDtypeStruct(flat.shape, F32),
        name="rotate",
    )(flat, coef)
    return out.reshape(data.shape)


def local(sizes, start_bands, potential, half_height, lower_bound, upper_bound, fermi_level):
    length = potential.shape[0]
    band_block = start_bands.shape[1]
    x_cells = start_bands.shape[2]
    group = sizes[1] * sizes[3]
    peers = sizes[0] * sizes[2]
    devices = group * peers
    bands = band_block * peers
    p = Plan(length, group, peers, bands, band_block)
    tables = build_tables(p)
    pairs = swap_pairs(sizes)
    cells_total = float(length**3)

    space = lax.ppermute(potential, AXES, pairs)
    space = pad_axis(space.transpose(2, 1, 0), 2, p.wide)

    box = start_bands.reshape(2, band_block, x_cells, length, length)
    box = pick(pick(box, 3, p), 4, p)
    height = pick(half_height, 1, p).astype(F32)
    stored = jnp.broadcast_to(height[None, None, :, :, None], box.shape[:4] + (p.fz - p.kept,))
    box = pad_axis(jnp.concatenate([box, stored], axis=4), 3, p.ky_all)
    box = lax.ppermute(box, AXES, pairs)
    box = box.reshape(2, band_block, x_cells, group, p.ky, p.fz)
    box = box.transpose(3, 4, 0, 5, 1, 2)
    box = exchange(box, GROUP)
    box = box.transpose(1, 2, 3, 4, 0, 5).reshape(p.ky, p.rows, band_block, length)
    box = pick(box, 3, p)
    field = pad_axis(box, 3, XP).reshape(p.ky, p.rows, p.lanes)

    member = lax.axis_index(GROUP)
    ky_index = member * p.ky + jnp.arange(p.ky, dtype=jnp.int32)
    x_index = jnp.arange(XP, dtype=jnp.int32)
    valid = (ky_index < p.kept)[:, None] & (jnp.tile(x_index, band_block) < p.kept)[None, :]
    heights = jnp.where(valid, field[:, p.kept, :], -1.0)
    fold = lambda k: jnp.where(k <= p.quarter, k, k - p.kept)
    squares = fold(ky_index)[:, None] ** 2 + jnp.tile(fold(x_index), band_block)[None, :] ** 2
    cols = jnp.stack([heights, squares.astype(F32)], axis=1)
    cols = pad_axis(cols, 1, 8)

    center = 0.5 * (upper_bound[0] + lower_bound[0])
    half_width = 0.5 * (upper_bound[0] - lower_bound[0])
    scal = jnp.stack([1.0 / half_width, center])

    previous, sent = z_stage(p, tables, scal, cols, field)
    current = previous
    for step in range(DEGREE):
        landed = exchange(sent, GROUP)
        middle = mid_stage(p, tables, landed, space)
        back = exchange(middle, GROUP)
        last = step == DEGREE - 1
        result = z_stage(
            p, tables, scal, cols, current, back, previous if step else None, fwd=not last
        )
        previous, current = current, result[0]
        if not last:
            sent = result[1]

    share = p.ky * p.fz // peers
    parts = current.reshape(p.ky, 2, p.fz, p.lanes).transpose(1, 0, 2, 3)
    parts = parts.reshape(2, peers, share, p.lanes).transpose(1, 0, 2, 3)
    everything = exchange(parts, PEERS)
    sums = gram_parts(p, everything)
    sums = jnp.pad(sums.reshape(-1), (0, round_up(sums.size, 1024) - sums.size))
    sums = collect(sums.reshape(-1, 128), AXES, devices).sum(axis=0).reshape(-1)
    sums = sums[: 2 * (2 * peers) ** 2 * band_block]
    gram_real, gram_imag = gram_matrices(p, sums)
    upper, lower = inverse_factor(gram_real, gram_imag)
    rotated = exchange(rotate(p, everything, upper, lower), PEERS)
    rotated = rotated.transpose(1, 0, 2, 3).reshape(2, p.ky, p.fz, p.lanes)
    rotated = rotated.transpose(1, 0, 2, 3).reshape(p.ky, p.rows, p.lanes)

    sent, kinetic_part = z_stage(p, tables, scal, cols, rotated, energy=True)
    landed = exchange(sent, GROUP)
    potential_part = mid_stage(p, tables, landed, space, energy=True)
    kinetic_sum = kinetic_part.reshape(-1, band_block, XP).sum(axis=(0, 2))
    partial = (kinetic_sum + potential_part.sum(axis=(1, 2)) / cells_total) / cells_total
    tile = jnp.broadcast_to(pad_axis(partial, 0, 128)[None], (8, 128))
    gathered = collect(tile, AXES, devices)[:, 0, :band_block]
    table = gathered.reshape(sizes + (band_block,)).sum(axis=(1, 3)).reshape(bands)
    weights = jax.nn.sigmoid((fermi_level[0] - table) / TEMPER)
    band_energy = (jnp.sum(weights * table) / float(bands)).reshape(1)
    first = lax.axis_index(BAND) * band_block
    energies = lax.dynamic_slice_in_dim(table, first, band_block, 0)

    box = rotated.reshape(p.ky, 2, p.fz, band_block, XP)[:, :, : p.kept, :, : p.kept]
    box = place(box, 4, p).reshape(p.ky, 2, p.kept, band_block, group, x_cells)
    box = exchange(box.transpose(4, 0, 1, 2, 3, 5), GROUP)
    box = box.transpose(2, 4, 5, 0, 1, 3)
    box = box.reshape(2, band_block, x_cells, p.ky_all, p.kept)[:, :, :, : p.kept]
    box = lax.ppermute(box, AXES, pairs)
    box = place(place(box, 4, p), 3, p)
    filtered = box.reshape(2, band_block, x_cells, length * length)
    return (filtered, energies, band_energy)


def solution(mesh):
    bands, slabs = mesh.shape["band"], mesh.shape["fft"]
    sizes = (bands // 2, 2, 2, slabs // 2)
    fine = Mesh(mesh.devices.reshape(sizes), AXES)
    placed = (P(None, BAND, FFT, None), P(None, None, FFT), P(FFT, None), P(), P(), P())
    return jax.shard_map(
        functools.partial(local, sizes),
        mesh=fine,
        in_specs=placed,
        out_specs=(P(None, BAND, FFT, None), P(BAND), P()),
        check_vma=False,
    )
```

```python
import functools

import jax
import jax.numpy as jnp
import numpy as np
from jax import lax
from jax.experimental import pallas as pl
from jax.experimental.pallas import tpu as pltpu
from jax.sharding import Mesh
from jax.sharding import PartitionSpec as P

DEGREE = 3
KIN_MAX = 12.0
TEMPER = 0.5
XP = 64
LANES = 2 * XP
KB = 8
BF = jnp.bfloat16
F32 = jnp.float32
AXES = ("bh", "bl", "fh", "ib", "dup")
BAND = ("bh", "bl")
FFT = ("fh", "ib", "dup")
SLABS = ("bl", "ib", "dup")
PEERS = ("bh", "fh", "ib")


def round_up(value, unit):
    return -(-value // unit) * unit


class Plan:
    def __init__(self, length, bands):
        self.length = length
        self.bands = bands
        self.quarter = length // 4
        self.kept = 2 * self.quarter + 1
        self.side = self.quarter + 1
        self.half = round_up(self.side, 4 * KB)
        self.blocks = self.half // KB
        self.both = 2 * self.half
        self.planes = length // 2
        self.wide = round_up(length, 128)


def split_np(table):
    high = np.asarray(table, np.float32).astype(BF)
    low = np.asarray(table - high.astype(np.float64), np.float32).astype(BF)
    return high, low


def left_table(table):
    high, low = split_np(table)
    return np.concatenate([high, high, low], axis=1)


def build_tables(p):
    length, mid = p.length, p.planes
    step = 2.0 * np.pi / length
    freq = np.zeros(p.both)
    live = np.zeros(p.both)
    freq[: p.side] = np.arange(p.side)
    live[: p.side] = 1.0
    freq[p.half + 1 : p.half + p.side] = -np.arange(1, p.side)
    live[p.half + 1 : p.half + p.side] = 1.0
    near = np.arange(mid)
    angle = step * ((near[:, None] * freq[None, :]) % length)
    cos, sin = np.cos(angle) * live, np.sin(angle) * live
    sin[0] = np.cos(step * ((mid * freq) % length)) * live
    unfold = np.concatenate([cos, sin], axis=0)
    size = np.arange(p.half)
    keep = (size < p.side)[:, None]

    def fold(order):
        turn = step * ((size[:, None] * order[None, :]) % length)
        return np.concatenate([np.cos(turn) * keep, np.sin(turn) * keep], axis=0)

    order_z = np.concatenate([near, length - 1 - near])
    order_y = np.concatenate([near, [mid], length - near[1:]])
    kx = np.concatenate([np.arange(p.side), np.arange(-p.quarter, 0)])
    turn = step * ((kx[:, None] * np.arange(length)[None, :]) % length)
    to_x = np.zeros((2, XP, 2, p.wide))
    to_x[0, : p.kept, 0, :length] = np.cos(turn)
    to_x[0, : p.kept, 1, :length] = np.sin(turn)
    to_x[1, : p.kept, 0, :length] = -np.sin(turn)
    to_x[1, : p.kept, 1, :length] = np.cos(turn)
    to_x = to_x.reshape(LANES, 2 * p.wide)
    high, low = split_np(to_x)
    back_high, back_low = split_np(np.ascontiguousarray(to_x.T))
    return {
        "unfold": left_table(unfold),
        "fold_z": left_table(fold(order_z)),
        "fold_y": left_table(fold(order_y)),
        "to_x": np.concatenate([high, high, low], axis=0),
        "from_x": np.concatenate([back_high, back_low], axis=1),
    }


def split(value):
    high = value.astype(BF)
    low = (value - high.astype(F32)).astype(BF)
    return high, low


def dot(a, b):
    return jnp.dot(a, b, preferred_element_type=F32)


def left_mul(table, value):
    high, low = split(value)
    return dot(table, jnp.concatenate([high, low, high], axis=0))


def half_sign(rows, sign):
    lane = lax.broadcasted_iota(jnp.int32, (rows, LANES), 1)
    return jnp.where(lane < XP, -sign, sign).astype(F32)


def cut(value, j):
    return value[:, j * LANES : (j + 1) * LANES]


def unfold_planes(table, columns):
    both = left_mul(table, jnp.concatenate(columns, axis=1))
    n = both.shape[0] // 2
    sign = half_sign(n, 1.0)
    first = lax.broadcasted_iota(jnp.int32, (n, LANES), 0) == 0
    out = []
    for j in range(len(columns)):
        here = cut(both, j)
        even, odd = here[:n], here[n:]
        turned = sign * pltpu.roll(odd, XP, 1)
        low = even + jnp.where(first, 0.0, turned)
        high = jnp.where(first, odd, even - turned)
        out.append((low, high))
    return out


def fold_planes(table, columns):
    both = left_mul(table, jnp.concatenate(columns, axis=1))
    n = both.shape[0] // 2
    sign = half_sign(n, 1.0)
    out = []
    for j in range(len(columns)):
        here = cut(both, j)
        turned = sign * pltpu.roll(here[n:], XP, 1)
        out.append((here[:n] - turned, here[:n] + turned))
    return out


def swap_if(first, a, b):
    return jnp.where(first, a, b), jnp.where(first, b, a)


def z_kernel(p, has_back, has_prev, has_field, has_fwd, has_energy, *refs):
    refs = list(refs)
    scal, cols, field = refs.pop(0), refs.pop(0), refs.pop(0)
    own_in = refs.pop(0) if has_back else None
    far_in = refs.pop(0) if has_back else None
    prev = refs.pop(0) if has_prev else None
    fold_z = refs.pop(0) if has_back else None
    unfold = refs.pop(0) if has_fwd else None
    out_field = refs.pop(0) if has_field else None
    out_own = refs.pop(0) if has_fwd else None
    out_far = refs.pop(0) if has_fwd else None
    out_energy = refs.pop(0) if has_energy else None
    first = scal[2] < 0.5
    index = lax.broadcasted_iota(jnp.int32, (p.both, LANES), 0)
    size = jnp.where(index < p.half, index, index - p.half)
    good = (size < p.side) & (index != p.half)
    distance = jnp.where(good, size, 2 * p.length).astype(F32)
    squared = (size * size).astype(F32)
    if has_back:
        columns = []
        for k in range(KB):
            own = own_in[0, pl.ds(k, p.planes, stride=KB), :]
            far = far_in[0, pl.ds(k, p.planes, stride=KB), :]
            columns.append(jnp.concatenate(swap_if(first, own, far), axis=0))
        moved = fold_planes(fold_z[...], columns)
    values = []
    total = 0.0
    for k in range(KB):
        inside = distance <= cols[k, 0:1, :]
        kinetic = (KIN_MAX / p.quarter**2) * (cols[k, 1:2, :] + squared)
        value = field[k]
        if has_back:
            spread = jnp.concatenate(moved[k], axis=0)
            applied = kinetic * value + (1.0 / p.length**3) * spread
            applied = jnp.where(inside, applied, 0.0)
            value = scal[0] * (applied - scal[1] * value)
            if has_prev:
                value = 2.0 * value - prev[k]
        else:
            value = jnp.where(inside, value, 0.0)
        if has_field:
            out_field[k] = value
        if has_energy:
            total = total + (kinetic * value * value).reshape(-1, 8, LANES).sum(axis=0)
        values.append(value)
    if has_energy:
        out_energy[0] = total
    if has_fwd:
        for k, (low, high) in enumerate(unfold_planes(unfold[...], values)):
            high = pltpu.roll(high, p.planes - 1, 0)
            own, far = swap_if(first, low, high)
            out_own[0, pl.ds(k, p.planes, stride=KB), :] = own
            out_far[0, pl.ds(k, p.planes, stride=KB), :] = far


def z_stage(p, tables, scal, cols, field, back=None, prev=None, fwd=True, energy=False):
    has_field = not energy
    plane = pl.BlockSpec((KB, p.both, LANES), lambda i: (i, 0, 0))
    chunk = pl.BlockSpec((1, p.planes * KB, LANES), lambda i: (i, 0, 0))
    whole = lambda a: pl.BlockSpec(a.shape, lambda i: (0,) * a.ndim)
    args = [scal, cols, field]
    specs = [
        pl.BlockSpec(memory_space=pltpu.SMEM),
        pl.BlockSpec((KB, 8, LANES), lambda i: (i, 0, 0)),
        plane,
    ]
    if back is not None:
        args += list(back)
        specs += [chunk, chunk]
    if prev is not None:
        args.append(prev)
        specs.append(plane)
    for name, used in (("fold_z", back is not None), ("unfold", fwd)):
        if used:
            args.append(jnp.asarray(tables[name]))
            specs.append(whole(args[-1]))
    outs, out_specs = [], []
    if has_field:
        outs.append(jax.ShapeDtypeStruct((p.half, p.both, LANES), F32))
        out_specs.append(plane)
    if fwd:
        outs += [jax.ShapeDtypeStruct((p.blocks, p.planes * KB, LANES), F32)] * 2
        out_specs += [chunk, chunk]
    if energy:
        outs.append(jax.ShapeDtypeStruct((p.blocks, 8, LANES), F32))
        out_specs.append(pl.BlockSpec((1, 8, LANES), lambda i: (i, 0, 0)))
    body = functools.partial(
        z_kernel, p, back is not None, prev is not None, has_field, fwd, energy
    )
    return pl.pallas_call(
        body,
        grid=(p.blocks,),
        in_specs=specs,
        out_specs=out_specs,
        out_shape=outs,
        name="z_stage",
    )(*args)


def mid_kernel(p, step, block, energy, scal, own_in, far_in, potential, unfold, to_x, *rest):
    if energy:
        (out,) = rest
    else:
        from_x, fold_y, out_own, out_far = rest
    length = p.length
    first = scal[2] < 0.5
    total = 0.0
    for start in range(0, step, block):
        columns = []
        for z in range(start, start + block):
            here = slice(z * KB, (z + 1) * KB)
            own = jnp.concatenate([own_in[k, here, :] for k in range(p.blocks)], axis=0)
            far = jnp.concatenate([far_in[k, here, :] for k in range(p.blocks)], axis=0)
            columns.append(jnp.concatenate(swap_if(first, own, far), axis=0))
        lined = [half for pair in unfold_planes(unfold[...], columns) for half in pair]
        high, low = split(jnp.concatenate(lined, axis=0))
        space = dot(jnp.concatenate([high, low, high], axis=1), to_x[...])
        local = potential[start : start + block].reshape(block * length, p.wide)
        if energy:
            real, imag = space[:, : p.wide], space[:, p.wide :]
            dens = local * (real * real + imag * imag)
            total = total + dens.reshape(-1, 8, p.wide).sum(axis=0)
            continue
        high, low = split(space * jnp.concatenate([local, local], axis=1))
        strong = dot(high, from_x[...])
        ready = strong[:, :LANES] + strong[:, LANES:] + dot(low, from_x[:, :LANES])
        columns = [ready[j * length : (j + 1) * length] for j in range(block)]
        for j, pair in enumerate(fold_planes(fold_y[...], columns)):
            here = slice((start + j) * KB, (start + j + 1) * KB)
            own, far = swap_if(first, *pair)
            for k in range(p.blocks):
                out_own[k, here, :] = own[k * KB : (k + 1) * KB]
                out_far[k, here, :] = far[k * KB : (k + 1) * KB]
    if energy:
        out[0] = total


def mid_stage(p, tables, scal, own, far, potential, energy=False):
    planes = potential.shape[0]
    step = max(d for d in range(1, 13) if planes % d == 0)
    block = max(d for d in range(1, 5) if step % d == 0)
    names = ["unfold", "to_x"] + ([] if energy else ["from_x", "fold_y"])
    args = [scal, own, far, potential] + [jnp.asarray(tables[n]) for n in names]
    chunk = pl.BlockSpec((p.blocks, step * KB, LANES), lambda i: (0, i, 0))
    specs = [
        pl.BlockSpec(memory_space=pltpu.SMEM),
        chunk,
        chunk,
        pl.BlockSpec((step, p.length, p.wide), lambda i: (i, 0, 0)),
    ]
    specs += [pl.BlockSpec(a.shape, lambda i: (0, 0)) for a in args[4:]]
    steps = planes // step
    if energy:
        outs = jax.ShapeDtypeStruct((steps, 8, p.wide), F32)
        out_specs = pl.BlockSpec((1, 8, p.wide), lambda i: (i, 0, 0))
    else:
        outs = [jax.ShapeDtypeStruct(own.shape, F32)] * 2
        out_specs = [chunk, chunk]
    return pl.pallas_call(
        functools.partial(mid_kernel, p, step, block, energy),
        grid=(steps,),
        in_specs=specs,
        out_specs=out_specs,
        out_shape=outs,
        name="mid_stage",
    )(*args)


def exchange(value, axes):
    return lax.all_to_all(value, axes, 0, 0, tiled=True)


def collect(value, axes, count):
    return exchange(jnp.broadcast_to(value[None], (count,) + value.shape), axes)


def swap_pairs(sizes):
    bh, bl, fh, fl = sizes
    number = lambda a, b, c, d: ((a * bl + b) * fh + c) * fl + d
    return [
        (number(a, b, c, d), number(a, c, b, d))
        for a in range(bh)
        for b in range(bl)
        for c in range(fh)
        for d in range(fl)
    ]


def pick(array, axis, p):
    lower = lax.slice_in_dim(array, 0, p.side, axis=axis)
    upper = lax.slice_in_dim(array, p.length - p.quarter, p.length, axis=axis)
    return jnp.concatenate([lower, upper], axis=axis)


def place(array, axis, p):
    lower = lax.slice_in_dim(array, 0, p.side, axis=axis)
    upper = lax.slice_in_dim(array, p.side, p.kept, axis=axis)
    shape = list(array.shape)
    shape[axis] = p.length - p.kept
    return jnp.concatenate([lower, jnp.zeros(tuple(shape), array.dtype), upper], axis=axis)


def pad_axis(array, axis, size, fill=0.0, front=False):
    widths = [(0, 0)] * array.ndim
    extra = size - array.shape[axis]
    widths[axis] = (extra, 0) if front else (0, extra)
    return jnp.pad(array, widths, constant_values=fill)


def gram_kernel(p, data, out):
    n = p.bands
    parts = [data[i] for i in range(n)]
    sign = half_sign(parts[0].shape[0], -1.0)
    turned = [sign * pltpu.roll(v, XP, 1) for v in parts]
    row = lax.broadcasted_iota(jnp.int32, out.shape, 0)
    lane = lax.broadcasted_iota(jnp.int32, out.shape, 1)
    acc = jnp.zeros(out.shape, F32)
    for i in range(n):
        for j in range(i, n):
            real = jnp.sum(jnp.sum(parts[i] * parts[j], axis=0, keepdims=True), axis=1, keepdims=True)
            here = ((row == i) & (lane == j)) | ((row == j) & (lane == i))
            here = here | ((row == n + i) & (lane == n + j)) | ((row == n + j) & (lane == n + i))
            acc = jnp.where(here, real, acc)
            if i == j:
                continue
            imag = jnp.sum(jnp.sum(parts[i] * turned[j], axis=0, keepdims=True), axis=1, keepdims=True)
            plus = ((row == n + i) & (lane == j)) | ((row == j) & (lane == n + i))
            minus = ((row == n + j) & (lane == i)) | ((row == i) & (lane == n + j))
            acc = jnp.where(plus, imag, jnp.where(minus, -imag, acc))
    out[...] = acc * (1.0 / p.length**3)


def rotate_kernel(p, data, terms, out):
    n = p.bands
    size = terms.shape[1]
    rows = lax.broadcasted_iota(jnp.int32, (size, 128), 0)
    lanes = lax.broadcasted_iota(jnp.int32, (size, 128), 1)
    work = jnp.sum(terms[...], axis=0) + jnp.where(lanes == rows + 2 * n, 1.0, 0.0)
    for k in range(2 * n):
        scale = 1.0 / jnp.sqrt(work[k : k + 1, k : k + 1])
        row = work[k : k + 1, :] * scale
        column = work[:, k : k + 1] * scale
        work = jnp.where(rows == k, row, work - jnp.where(rows > k, column * row, 0.0))
    parts = [data[i] for i in range(n)]
    sign = half_sign(parts[0].shape[0], 1.0)
    turned = [sign * pltpu.roll(v, XP, 1) for v in parts]
    for b in range(n):
        acc = None
        for i in range(n):
            term = parts[i] * work[b : b + 1, 2 * n + i : 2 * n + i + 1]
            term = term + turned[i] * work[b : b + 1, 3 * n + i : 3 * n + i + 1]
            acc = term if acc is None else acc + term
        out[b] = acc


def call(body, shape, name, *args):
    vmem = pl.BlockSpec(memory_space=pltpu.VMEM)
    return pl.pallas_call(
        body,
        in_specs=[vmem] * len(args),
        out_specs=vmem,
        out_shape=jax.ShapeDtypeStruct(shape, F32),
        name=name,
    )(*args)


def local(sizes, start_bands, potential, half_height, lower_bound, upper_bound, fermi_level):
    length = potential.shape[0]
    band_block = start_bands.shape[1]
    x_cells = start_bands.shape[2]
    copies = sizes[4]
    group = sizes[1] * sizes[3] * copies
    peers = sizes[0] * sizes[2] * sizes[3]
    devices = peers * sizes[1] * copies
    p = Plan(length, peers)
    tables = build_tables(p)
    pairs = swap_pairs(sizes[:3] + (sizes[3] * copies,))
    cells_total = float(length**3)
    low = lax.axis_index("bl")
    copy = lax.axis_index("dup")

    deep = p.kept + 1
    flat = round_up(p.side * deep, 128)
    box = start_bands.reshape(2, band_block, x_cells, length, length)
    box = pick(pick(box, 3, p), 4, p)
    height = pick(half_height, 1, p).astype(F32)
    stored = jnp.broadcast_to(height[None, None, :, :, None], box.shape[:4] + (1,))
    box = pad_axis(jnp.concatenate([box, stored], axis=4), 3, 2 * p.side)
    box = box.reshape(2, band_block, x_cells, 2, p.side * deep).transpose(3, 1, 0, 2, 4)
    box = pad_axis(box, 4, flat)
    box = lax.ppermute(box.reshape(2, band_block, -1, 128), AXES, pairs)
    space = potential.transpose(2, 1, 0)
    space = jnp.concatenate([space[:, : p.planes + 1], lax.rev(space[:, p.planes + 1 :], (1,))], 1)
    space = lax.ppermute(space.reshape(-1, 128), AXES, pairs)
    box = jnp.broadcast_to(box[:, :, None], box.shape[:2] + (copies,) + box.shape[2:])
    box = exchange(box.reshape((group,) + box.shape[3:]), SLABS)
    space = collect(space, ("ib", "dup"), sizes[3] * copies)
    space = space.reshape(p.planes, length, length)
    space = pad_axis(jnp.where(low == 0, space, lax.rev(space, (0,))), 2, p.wide)
    some = p.planes // copies
    space_part = lax.dynamic_slice_in_dim(space, copy * some, some, 0)

    box = box.reshape(group, 2, x_cells, flat)[..., : p.side * deep]
    box = box.reshape(group, 2, x_cells, p.side, deep).transpose(3, 4, 1, 0, 2)
    box = pick(box.reshape(p.side, deep, 2, length), 3, p)
    box = jnp.where(low == 0, box, lax.rev(box, (0,)))
    heights = box[:, p.kept, 0]
    box = pad_axis(box, 3, XP).reshape(p.side, deep, LANES)
    minus = pad_axis(lax.rev(box[:, p.side : p.kept], (1,)), 1, p.side, front=True)
    box = jnp.concatenate([pad_axis(box[:, : p.side], 1, p.half), pad_axis(minus, 1, p.half)], 1)
    field = pad_axis(box, 0, p.half)

    y_index = jnp.arange(p.side, dtype=jnp.int32)
    x_index = jnp.arange(p.kept, dtype=jnp.int32)
    x_index = jnp.where(x_index <= p.quarter, x_index, x_index - p.kept)
    heights = jnp.where((low == 0) | (y_index > 0)[:, None], heights, -1.0)
    squares = (y_index[:, None] ** 2 + x_index[None, :] ** 2).astype(F32)
    spread = lambda v, fill: jnp.tile(
        pad_axis(pad_axis(v, 1, XP, fill=fill), 0, p.half, fill=fill), (1, 2)
    )
    cols = pad_axis(jnp.stack([spread(heights, -1.0), spread(squares, 0.0)], axis=1), 1, 8)

    center = 0.5 * (upper_bound[0] + lower_bound[0])
    half_width = 0.5 * (upper_bound[0] - lower_bound[0])
    scal = jnp.stack([1.0 / half_width, center, low.astype(F32)])

    other = [(0, 1), (1, 0)]
    previous = None
    current, own, far = z_stage(p, tables, scal, cols, field)
    for step in range(DEGREE):
        last = step == DEGREE - 1
        far = lax.ppermute(far, "bl", other)
        own, far = mid_stage(p, tables, scal, own, far, space)
        far = lax.ppermute(far, "bl", other)
        result = z_stage(p, tables, scal, cols, current, (own, far), previous, fwd=not last)
        previous, current = current, result[0]
        if not last:
            own, far = result[1:]

    share = p.half * p.both // (copies * peers)
    parts = current.reshape(copies, peers, share, LANES)
    parts = lax.dynamic_index_in_dim(parts, copy, 0, keepdims=False)
    everything = exchange(parts, PEERS)
    size = round_up(2 * p.bands, 8)
    terms = call(functools.partial(gram_kernel, p), (size, 128), "gram", everything)
    terms = collect(terms, AXES, devices)
    rotated = call(
        functools.partial(rotate_kernel, p), everything.shape, "rotate", everything, terms
    )
    rotated = jnp.broadcast_to(rotated[:, None], (peers, copies, share, LANES))
    rotated = exchange(rotated.reshape(peers * copies, share, LANES), PEERS + ("dup",))
    rotated = rotated.reshape(peers, copies, share, LANES).transpose(1, 0, 2, 3)
    rotated = rotated.reshape(p.half, p.both, LANES)

    own, far, kinetic_part = z_stage(p, tables, scal, cols, rotated, energy=True)
    far = lax.ppermute(far, "bl", other)
    rows = lambda v: lax.dynamic_slice_in_dim(v, copy * some * KB, some * KB, 1)
    potential_part = mid_stage(p, tables, scal, rows(own), rows(far), space_part, energy=True)
    partial = kinetic_part.sum() / copies + potential_part.sum() / cells_total
    tile = jnp.broadcast_to(partial / cells_total, (8, 128))
    gathered = collect(tile, AXES, devices)[:, 0, 0]
    table = gathered.reshape(sizes).sum(axis=(1, 4)).reshape(p.bands)
    weights = jax.nn.sigmoid((fermi_level[0] - table) / TEMPER)
    band_energy = (jnp.sum(weights * table) / float(p.bands)).reshape(1)
    energies = lax.dynamic_slice_in_dim(table, lax.axis_index(BAND) * band_block, band_block, 0)

    count = -(-p.side // copies)
    flat = round_up(count * p.kept, 128)
    box = rotated[: p.side]
    box = pad_axis(jnp.where(low == 0, box, lax.rev(box, (0,))), 0, count * copies)
    box = lax.dynamic_slice_in_dim(box, copy * count, count, 0)
    minus = lax.rev(box[:, p.half + 1 : p.half + p.side], (1,))
    box = jnp.concatenate([box[:, : p.side], minus], axis=1)
    box = place(box.reshape(count, p.kept, 2, XP)[..., : p.kept], 3, p)
    box = box.reshape(count, p.kept, 2, group, x_cells).transpose(3, 2, 4, 0, 1)
    box = pad_axis(box.reshape(group, 2, x_cells, count * p.kept), 3, flat)
    box = exchange(box.reshape(group, -1, 128), SLABS)
    box = lax.ppermute(box, AXES, pairs)
    box = box.reshape(sizes[1], band_block, copies, 2, x_cells, flat)[..., : count * p.kept]
    box = box.reshape(sizes[1], band_block, copies, 2, x_cells, count, p.kept)
    box = box.transpose(3, 1, 4, 0, 2, 5, 6)
    box = box.reshape(2, band_block, x_cells, sizes[1], copies * count, p.kept)
    box = jnp.concatenate([box[:, :, :, 0, : p.side], box[:, :, :, 1, : p.quarter]], axis=3)
    box = place(place(box, 4, p), 3, p)
    filtered = box.reshape(2, band_block, x_cells, length * length)
    return (filtered, energies, band_energy)


def solution(mesh):
    bands, slabs = mesh.shape["band"], mesh.shape["fft"]

    def body(start_bands, *rest):
        block = start_bands.shape[1] // bands
        sizes = (bands // 2, 2, 2, block, slabs // (2 * block))
        fine = Mesh(mesh.devices.reshape(sizes), AXES)
        placed = (P(None, BAND, FFT, None), P(None, None, FFT), P(FFT, None), P(), P(), P())
        return jax.shard_map(
            functools.partial(local, sizes),
            mesh=fine,
            in_specs=placed,
            out_specs=(P(None, BAND, FFT, None), P(BAND), P()),
            check_vma=False,
        )(start_bands, *rest)

    return body
```

```python
import functools

import jax
import jax.numpy as jnp
import numpy as np
from jax import lax
from jax.experimental import pallas as pl
from jax.experimental.pallas import tpu as pltpu
from jax.sharding import Mesh
from jax.sharding import PartitionSpec as P

DEGREE = 3
KIN_MAX = 12.0
TEMPER = 0.5
XP = 64
LANES = 2 * XP
KB = 8
BF = jnp.bfloat16
F32 = jnp.float32
AXES = ("bh", "bl", "hi", "dup", "bc", "ib")
BAND = ("bh", "bl")
FFT = ("hi", "dup", "bc", "ib")
QUARTER = ("dup", "bc", "ib")
PEERS = ("bh", "bc", "ib")


def round_up(value, unit):
    return -(-value // unit) * unit


class Plan:
    def __init__(self, length, bands):
        self.length = length
        self.bands = bands
        self.quarter = length // 4
        self.kept = 2 * self.quarter + 1
        self.side = self.quarter + 1
        self.half = round_up(self.side, 4 * KB)
        self.blocks = self.half // KB
        self.both = 2 * self.half
        self.planes = length // 2
        self.wide = round_up(length, 128)
        self.group_y = 4


def split_np(table):
    high = np.asarray(table, np.float32).astype(BF)
    low = np.asarray(table - high.astype(np.float64), np.float32).astype(BF)
    return high, low


def left_table(table):
    high, low = split_np(table)
    return np.concatenate([high, high, low], axis=1)


def build_tables(p):
    length, mid = p.length, p.planes
    step = 2.0 * np.pi / length
    freq = np.zeros(p.both)
    live = np.zeros(p.both)
    freq[: p.side] = np.arange(p.side)
    live[: p.side] = 1.0
    freq[p.half + 1 : p.half + p.side] = -np.arange(1, p.side)
    live[p.half + 1 : p.half + p.side] = 1.0
    near = np.arange(mid)
    angle = step * ((near[:, None] * freq[None, :]) % length)
    cos, sin = np.cos(angle) * live, np.sin(angle) * live
    sin[0] = np.cos(step * ((mid * freq) % length)) * live
    unfold = np.concatenate([cos, sin], axis=0)
    size = np.arange(p.half)
    keep = (size < p.side)[:, None]

    def fold(order):
        turn = step * ((size[:, None] * order[None, :]) % length)
        return np.concatenate([np.cos(turn) * keep, np.sin(turn) * keep], axis=0)

    order_z = np.concatenate([near, length - 1 - near])
    order_y = np.concatenate([near, [mid], length - near[1:]])
    kx = np.concatenate([np.arange(p.side), np.arange(-p.quarter, 0)])
    turn = step * ((kx[:, None] * np.arange(length)[None, :]) % length)
    to_x = np.zeros((2, XP, 2, p.wide))
    to_x[0, : p.kept, 0, :length] = np.cos(turn)
    to_x[0, : p.kept, 1, :length] = np.sin(turn)
    to_x[1, : p.kept, 0, :length] = -np.sin(turn)
    to_x[1, : p.kept, 1, :length] = np.cos(turn)
    to_x = to_x.reshape(LANES, 2 * p.wide)
    high, low = split_np(to_x)
    back_high, back_low = split_np(np.ascontiguousarray(to_x.T))
    def land(count, where):
        table = np.zeros((count, 2 * p.half, p.group_y, length))
        for u in range(count):
            t = where(u)
            if 0 <= t < p.group_y:
                table[u, np.arange(p.side), t, np.arange(p.side)] = 1.0
                far = np.arange(1, p.side)
                table[u, p.half + far, t, length - far] = 1.0
        table = table.reshape(count * 2 * p.half, p.group_y * length)
        return np.concatenate([table, table], axis=0).astype(BF)

    return {
        "land_plus": land(p.group_y, lambda u: u),
        "land_minus": land(p.group_y + 2, lambda u: p.group_y - u),
        "unfold": left_table(unfold),
        "fold_z": left_table(fold(order_z)),
        "fold_y": left_table(fold(order_y)),
        "to_x": np.concatenate([high, high, low], axis=0),
        "from_x": np.concatenate([back_high, back_low], axis=1),
    }


def split(value):
    high = value.astype(BF)
    low = (value - high.astype(F32)).astype(BF)
    return high, low


def dot(a, b):
    return jnp.dot(a, b, preferred_element_type=F32)


def left_mul(table, value):
    high, low = split(value)
    return dot(table, jnp.concatenate([high, low, high], axis=0))


def half_sign(rows, sign):
    lane = lax.broadcasted_iota(jnp.int32, (rows, LANES), 1)
    return jnp.where(lane < XP, -sign, sign).astype(F32)


def cut(value, j):
    return value[:, j * LANES : (j + 1) * LANES]


def unfold_planes(table, columns):
    both = left_mul(table, jnp.concatenate(columns, axis=1))
    n = both.shape[0] // 2
    sign = half_sign(n, 1.0)
    first = lax.broadcasted_iota(jnp.int32, (n, LANES), 0) == 0
    out = []
    for j in range(len(columns)):
        here = cut(both, j)
        even, odd = here[:n], here[n:]
        turned = sign * pltpu.roll(odd, XP, 1)
        low = even + jnp.where(first, 0.0, turned)
        high = jnp.where(first, odd, even - turned)
        out.append((low, high))
    return out


def fold_planes(table, columns):
    both = left_mul(table, jnp.concatenate(columns, axis=1))
    n = both.shape[0] // 2
    sign = half_sign(n, 1.0)
    out = []
    for j in range(len(columns)):
        here = cut(both, j)
        turned = sign * pltpu.roll(here[n:], XP, 1)
        out.append((here[:n] - turned, here[:n] + turned))
    return out


def swap_if(first, a, b):
    return jnp.where(first, a, b), jnp.where(first, b, a)


def z_kernel(p, has_back, has_prev, has_field, has_fwd, has_energy, *refs):
    refs = list(refs)
    scal, cols, field = refs.pop(0), refs.pop(0), refs.pop(0)
    own_in = refs.pop(0) if has_back else None
    far_in = refs.pop(0) if has_back else None
    prev = refs.pop(0) if has_prev else None
    fold_z = refs.pop(0) if has_back else None
    unfold = refs.pop(0) if has_fwd else None
    out_field = refs.pop(0) if has_field else None
    out_own = refs.pop(0) if has_fwd else None
    out_far = refs.pop(0) if has_fwd else None
    out_energy = refs.pop(0) if has_energy else None
    first = scal[2] < 0.5
    index = lax.broadcasted_iota(jnp.int32, (p.both, LANES), 0)
    size = jnp.where(index < p.half, index, index - p.half)
    good = (size < p.side) & (index != p.half)
    distance = jnp.where(good, size, 2 * p.length).astype(F32)
    squared = (size * size).astype(F32)
    if has_back:
        columns = []
        for k in range(KB):
            own = own_in[0, pl.ds(k, p.planes, stride=KB), :]
            far = far_in[0, pl.ds(k, p.planes, stride=KB), :]
            columns.append(jnp.concatenate(swap_if(first, own, far), axis=0))
        moved = fold_planes(fold_z[...], columns)
    values = []
    total = 0.0
    for k in range(KB):
        inside = distance <= cols[k, 0:1, :]
        kinetic = (KIN_MAX / p.quarter**2) * (cols[k, 1:2, :] + squared)
        value = field[k]
        if has_back:
            spread = jnp.concatenate(moved[k], axis=0)
            applied = kinetic * value + (1.0 / p.length**3) * spread
            applied = jnp.where(inside, applied, 0.0)
            value = scal[0] * (applied - scal[1] * value)
            if has_prev:
                value = 2.0 * value - prev[k]
        else:
            value = jnp.where(inside, value, 0.0)
        if has_field:
            out_field[k] = value
        if has_energy:
            total = total + (kinetic * value * value).reshape(-1, 8, LANES).sum(axis=0)
        values.append(value)
    if has_energy:
        out_energy[0] = total
    if has_fwd:
        for k, (low, high) in enumerate(unfold_planes(unfold[...], values)):
            high = pltpu.roll(high, p.planes - 1, 0)
            own, far = swap_if(first, low, high)
            out_own[0, pl.ds(k, p.planes, stride=KB), :] = own
            out_far[0, pl.ds(k, p.planes, stride=KB), :] = far


def z_stage(p, tables, scal, cols, field, back=None, prev=None, fwd=True, energy=False):
    has_field = not energy
    plane = pl.BlockSpec((KB, p.both, LANES), lambda i: (i, 0, 0))
    chunk = pl.BlockSpec((1, p.planes * KB, LANES), lambda i: (i, 0, 0))
    whole = lambda a: pl.BlockSpec(a.shape, lambda i: (0,) * a.ndim)
    args = [scal, cols, field]
    specs = [
        pl.BlockSpec(memory_space=pltpu.SMEM),
        pl.BlockSpec((KB, 8, LANES), lambda i: (i, 0, 0)),
        plane,
    ]
    if back is not None:
        args += list(back)
        specs += [chunk, chunk]
    if prev is not None:
        args.append(prev)
        specs.append(plane)
    for name, used in (("fold_z", back is not None), ("unfold", fwd)):
        if used:
            args.append(jnp.asarray(tables[name]))
            specs.append(whole(args[-1]))
    outs, out_specs = [], []
    if has_field:
        outs.append(jax.ShapeDtypeStruct((p.half, p.both, LANES), F32))
        out_specs.append(plane)
    if fwd:
        outs += [jax.ShapeDtypeStruct((p.blocks, p.planes * KB, LANES), F32)] * 2
        out_specs += [chunk, chunk]
    if energy:
        outs.append(jax.ShapeDtypeStruct((p.blocks, 8, LANES), F32))
        out_specs.append(pl.BlockSpec((1, 8, LANES), lambda i: (i, 0, 0)))
    body = functools.partial(
        z_kernel, p, back is not None, prev is not None, has_field, fwd, energy
    )
    return pl.pallas_call(
        body,
        grid=(p.blocks,),
        in_specs=specs,
        out_specs=out_specs,
        out_shape=outs,
        name="z_stage",
    )(*args)


def mid_kernel(p, step, block, energy, scal, own_in, far_in, potential, unfold, to_x, *rest):
    if energy:
        (out,) = rest
    else:
        from_x, fold_y, out_own, out_far = rest
    length = p.length
    first = scal[2] < 0.5
    total = 0.0
    for start in range(0, step, block):
        columns = []
        for z in range(start, start + block):
            here = slice(z * KB, (z + 1) * KB)
            own = jnp.concatenate([own_in[k, here, :] for k in range(p.blocks)], axis=0)
            far = jnp.concatenate([far_in[k, here, :] for k in range(p.blocks)], axis=0)
            columns.append(jnp.concatenate(swap_if(first, own, far), axis=0))
        lined = [half for pair in unfold_planes(unfold[...], columns) for half in pair]
        high, low = split(jnp.concatenate(lined, axis=0))
        space = dot(jnp.concatenate([high, low, high], axis=1), to_x[...])
        local = potential[start : start + block].reshape(block * length, p.wide)
        if energy:
            real, imag = space[:, : p.wide], space[:, p.wide :]
            dens = local * (real * real + imag * imag)
            total = total + dens.reshape(-1, 8, p.wide).sum(axis=0)
            continue
        high, low = split(space * jnp.concatenate([local, local], axis=1))
        strong = dot(high, from_x[...])
        ready = strong[:, :LANES] + strong[:, LANES:] + dot(low, from_x[:, :LANES])
        columns = [ready[j * length : (j + 1) * length] for j in range(block)]
        for j, pair in enumerate(fold_planes(fold_y[...], columns)):
            here = slice((start + j) * KB, (start + j + 1) * KB)
            own, far = swap_if(first, *pair)
            for k in range(p.blocks):
                out_own[k, here, :] = own[k * KB : (k + 1) * KB]
                out_far[k, here, :] = far[k * KB : (k + 1) * KB]
    if energy:
        out[0] = total


def mid_stage(p, tables, scal, own, far, potential, energy=False):
    planes = potential.shape[0]
    step = max(d for d in range(1, 13) if planes % d == 0)
    block = max(d for d in range(1, 5) if step % d == 0)
    names = ["unfold", "to_x"] + ([] if energy else ["from_x", "fold_y"])
    args = [scal, own, far, potential] + [jnp.asarray(tables[n]) for n in names]
    chunk = pl.BlockSpec((p.blocks, step * KB, LANES), lambda i: (0, i, 0))
    specs = [
        pl.BlockSpec(memory_space=pltpu.SMEM),
        chunk,
        chunk,
        pl.BlockSpec((step, p.length, p.wide), lambda i: (i, 0, 0)),
    ]
    specs += [pl.BlockSpec(a.shape, lambda i: (0, 0)) for a in args[4:]]
    steps = planes // step
    if energy:
        outs = jax.ShapeDtypeStruct((steps, 8, p.wide), F32)
        out_specs = pl.BlockSpec((1, 8, p.wide), lambda i: (i, 0, 0))
    else:
        outs = [jax.ShapeDtypeStruct(own.shape, F32)] * 2
        out_specs = [chunk, chunk]
    return pl.pallas_call(
        functools.partial(mid_kernel, p, step, block, energy),
        grid=(steps,),
        in_specs=specs,
        out_specs=out_specs,
        out_shape=outs,
        name="mid_stage",
    )(*args)


def exchange(value, axes):
    return lax.all_to_all(value, axes, 0, 0, tiled=True)


def collect(value, axes, count):
    return exchange(jnp.broadcast_to(value[None], (count,) + value.shape), axes)


def swap_pairs(sizes):
    bh, bl, fh, fl = sizes
    number = lambda a, b, c, d: ((a * bl + b) * fh + c) * fl + d
    return [
        (number(a, b, c, d), number(a, c, b, d))
        for a in range(bh)
        for b in range(bl)
        for c in range(fh)
        for d in range(fl)
    ]


def pick(array, axis, p):
    lower = lax.slice_in_dim(array, 0, p.side, axis=axis)
    upper = lax.slice_in_dim(array, p.length - p.quarter, p.length, axis=axis)
    return jnp.concatenate([lower, upper], axis=axis)


def pad_axis(array, axis, size, fill=0.0, front=False):
    widths = [(0, 0)] * array.ndim
    extra = size - array.shape[axis]
    widths[axis] = (extra, 0) if front else (0, extra)
    return jnp.pad(array, widths, constant_values=fill)


def gram_kernel(p, scal, data, applied, out):
    n = p.bands
    parts = [data[i] for i in range(n)]
    shape = parts[0].shape
    sign = half_sign(shape[0], -1.0)
    lane = lax.broadcasted_iota(jnp.int32, out.shape, 1)
    acc = jnp.zeros(out.shape, F32)
    for base, source in ((0, data), (2, applied)):
        for j in range(n):
            value = source[j]
            for kind, right in ((0, value), (1, sign * pltpu.roll(value, XP, 1))):
                rows = []
                for i in range(n):
                    product = (parts[i] * right).reshape(-1, 8, LANES).sum(axis=0)
                    rows.append(jnp.sum(product, axis=0, keepdims=True))
                total = jnp.sum(jnp.concatenate(rows, axis=0), axis=1, keepdims=True)
                acc = jnp.where(lane == (base + kind) * n + j, total, acc)
    out[...] = acc * (scal[3] / p.length**3)


def embed(p, tile, base):
    n = p.bands
    lane = lax.broadcasted_iota(jnp.int32, tile.shape, 1)
    real = pltpu.roll(tile, (128 - base * n) % 128, 1)
    top = jnp.where(lane < n, real, jnp.where(lane < 2 * n, -real, 0.0))
    bottom = jnp.where(
        lane < n,
        pltpu.roll(tile, 128 - (base + 1) * n, 1),
        jnp.where(lane < 2 * n, pltpu.roll(tile, (128 - (base - 1) * n) % 128, 1), 0.0),
    )
    return jnp.concatenate([top, bottom], axis=0)


def rotate_kernel(p, runs, x_cells, data, terms, out, energies, turned_ref):
    n = p.bands
    tile = jnp.sum(terms[...], axis=0)
    size = 2 * n
    rows = lax.broadcasted_iota(jnp.int32, (size, 128), 0)
    lanes = lax.broadcasted_iota(jnp.int32, (size, 128), 1)
    work = embed(p, tile, 0) + jnp.where(lanes == rows + size, 1.0, 0.0)
    for k in range(size):
        scale = 1.0 / jnp.sqrt(work[k : k + 1, k : k + 1])
        row = work[k : k + 1, :] * scale
        column = work[:, k : k + 1] * scale
        work = jnp.where(rows == k, row, work - jnp.where(rows > k, column * row, 0.0))
    weight = pltpu.roll(work, 128 - size, 1)[:n]
    projected = embed(p, tile, 2)
    moved = jnp.zeros((n, 128), F32)
    for k in range(size):
        moved = moved + weight[:, k : k + 1] * projected[k : k + 1, :]
    product = jnp.where(lanes[:n] < size, moved * weight, 0.0)
    energies[...] = jnp.broadcast_to(jnp.sum(product, axis=1, keepdims=True), energies.shape)
    out[...] = jnp.zeros(out.shape, F32)
    parts = [data[i] for i in range(n)]
    sign = half_sign(parts[0].shape[0], 1.0)
    turned = [sign * pltpu.roll(v, XP, 1) for v in parts]
    block = out.shape[2] // (2 * x_cells)
    for b in range(n):
        acc = None
        for i in range(n):
            term = parts[i] * weight[b : b + 1, i : i + 1]
            term = term + turned[i] * weight[b : b + 1, n + i : n + i + 1]
            acc = term if acc is None else acc + term
        turned_ref[b] = acc.T
        for part in range(2):
            base = (part * block + b % block) * x_cells
            for slab, offset, start, count in runs:
                here = turned_ref[b, pl.ds(part * XP + start, count), :]
                out[b // block, slab, pl.ds(base + offset, count), :] = here


def land_kernel(p, order, landed, plus, minus, out, keep_ref):
    rows = landed.shape[1]
    g = p.group_y
    pair = lambda side, j: landed[order(side, j // 2)]
    span = g * p.length
    lower = -(-p.side // g)
    upper = p.quarter // g

    def place(side, starts, count, table):
        windows = []
        for start in starts:
            windows.append(jnp.concatenate([pair(side, start + u) for u in range(0, count, 2)], axis=1))
        high, low = split(jnp.concatenate(windows, axis=0))
        return dot(jnp.concatenate([high, low], axis=1), table[...])

    keep_ref[: lower * rows] = place(0, [g * i for i in range(lower)], g, plus)
    top = [p.quarter - g - g * i for i in range(upper)]
    keep_ref[lower * rows : (lower + upper) * rows] = place(1, top, g + 2, minus)
    parts, block, x_cells, whole = out.shape
    first = (p.length - p.quarter) * p.length
    for part in range(parts):
        for i in range(block):
            out[part, i, :, lower * span : first] = jnp.zeros(
                (x_cells, first - lower * span), F32
            )
            base = (part * block + i) * x_cells
            for w in range(lower + upper):
                at = w * span if w < lower else first + (w - lower) * span
                here = keep_ref[pl.ds(w * rows + base, x_cells), :]
                out[part, i, :, at : at + span] = here


def kept_runs(p, x_cells):
    place = [k if k <= p.quarter else p.length - p.kept + k for k in range(p.kept)]
    runs = []
    for k, x in enumerate(place):
        slab, offset = divmod(x, x_cells)
        if runs and runs[-1][0] == slab and runs[-1][1] + runs[-1][3] == offset:
            runs[-1][3] += 1
        else:
            runs.append([slab, offset, k, 1])
    return runs


def local(sizes, start_bands, potential, half_height, lower_bound, upper_bound, fermi_level):
    length = potential.shape[0]
    band_block = start_bands.shape[1]
    x_cells = start_bands.shape[2]
    bh, bl, hi, dup, bc, ib = sizes
    copies = hi * dup
    slabs = copies * bc * ib
    peers = bh * bc * ib
    devices = peers * bl * copies
    p = Plan(length, peers)
    tables = build_tables(p)
    cells_total = float(length**3)
    low = lax.axis_index("bl")
    copy = lax.axis_index(("hi", "dup"))
    other = [(0, 1), (1, 0)]

    space = potential.transpose(2, 1, 0)
    space = jnp.concatenate([space[:, : p.planes + 1], lax.rev(space[:, p.planes + 1 :], (1,))], 1)
    space = lax.ppermute(space.reshape(-1, 128), AXES, swap_pairs((bh, bl, hi, slabs // hi)))
    deep = p.kept + 1
    flat = round_up(p.side * deep, 128)
    box = start_bands.reshape(2, band_block, x_cells, length, length)
    box = pick(pick(box, 3, p), 4, p)
    height = pick(half_height, 1, p).astype(F32)
    stored = jnp.broadcast_to(height[None, None, :, :, None], box.shape[:4] + (1,))
    box = pad_axis(jnp.concatenate([box, stored], axis=4), 3, 2 * p.side)
    box = box.reshape(2, band_block, x_cells, 2, p.side * deep).transpose(3, 1, 0, 2, 4)
    box = pad_axis(box, 4, flat).reshape(2, band_block, -1, 128)
    mine = jnp.where(low == 0, box[0], box[1])
    away = lax.ppermute(jnp.where(low == 0, box[1], box[0]), "bl", other)
    box = jnp.where(low == 0, jnp.stack([mine, away]), jnp.stack([away, mine]))
    box = jnp.broadcast_to(box[None], (copies,) + box.shape)
    box = exchange(box.reshape((slabs,) + box.shape[3:]), FFT)
    space = collect(space, QUARTER, slabs // hi)
    space = space.reshape(p.planes, length, length)
    space = pad_axis(jnp.where(low == 0, space, lax.rev(space, (0,))), 2, p.wide)

    box = box.reshape(slabs, 2, x_cells, flat)[..., : p.side * deep]
    box = box.reshape(slabs, 2, x_cells, p.side, deep).transpose(3, 4, 1, 0, 2)
    box = pick(box.reshape(p.side, deep, 2, length), 3, p)
    box = jnp.where(low == 0, box, lax.rev(box, (0,)))
    heights = box[:, p.kept, 0]
    box = pad_axis(box, 3, XP).reshape(p.side, deep, LANES)
    minus = pad_axis(lax.rev(box[:, p.side : p.kept], (1,)), 1, p.side, front=True)
    box = jnp.concatenate([pad_axis(box[:, : p.side], 1, p.half), pad_axis(minus, 1, p.half)], 1)
    field = pad_axis(box, 0, p.half)

    y_index = jnp.arange(p.side, dtype=jnp.int32)
    x_index = jnp.arange(p.kept, dtype=jnp.int32)
    x_index = jnp.where(x_index <= p.quarter, x_index, x_index - p.kept)
    heights = jnp.where((low == 0) | (y_index > 0)[:, None], heights, -1.0)
    squares = (y_index[:, None] ** 2 + x_index[None, :] ** 2).astype(F32)
    spread = lambda v, fill: jnp.tile(
        pad_axis(pad_axis(v, 1, XP, fill=fill), 0, p.half, fill=fill), (1, 2)
    )
    cols = pad_axis(jnp.stack([spread(heights, -1.0), spread(squares, 0.0)], axis=1), 1, 8)

    share_y = max(2, p.half // (copies * peers))
    in_use = p.half // (share_y * peers)
    counted = (copy < in_use).astype(F32)
    center = 0.5 * (upper_bound[0] + lower_bound[0])
    half_width = 0.5 * (upper_bound[0] - lower_bound[0])
    scal = jnp.stack([1.0 / half_width, center, low.astype(F32), counted])
    plain = jnp.stack([jnp.ones((), F32), jnp.zeros((), F32), low.astype(F32), counted])

    def take_share(value):
        parts = value.reshape(in_use, peers, share_y * p.both, LANES)
        parts = lax.dynamic_index_in_dim(parts, copy % in_use, 0, keepdims=False)
        return exchange(parts, PEERS)

    previous = None
    current, own, far = z_stage(p, tables, scal, cols, field)
    for step in range(DEGREE + 1):
        far = lax.ppermute(far, "bl", other)
        own, far = mid_stage(p, tables, scal, own, far, space)
        far = lax.ppermute(far, "bl", other)
        if step < DEGREE:
            result = z_stage(p, tables, scal, cols, current, (own, far), previous)
            previous, current = current, result[0]
            own, far = result[1:]
    everything = take_share(current)
    (applied,) = z_stage(p, tables, plain, cols, current, (own, far), fwd=False)
    applied = take_share(applied)

    smem = pl.BlockSpec(memory_space=pltpu.SMEM)
    vmem = pl.BlockSpec(memory_space=pltpu.VMEM)
    terms = pl.pallas_call(
        functools.partial(gram_kernel, p),
        in_specs=[smem, vmem, vmem],
        out_specs=vmem,
        out_shape=jax.ShapeDtypeStruct((p.bands, 128), F32),
        name="gram",
    )(scal, everything, applied)
    terms = collect(terms, AXES, devices)
    chunk = (bh * bl, slabs, 2 * band_block * x_cells, share_y * p.both)
    rotated, table = pl.pallas_call(
        functools.partial(rotate_kernel, p, kept_runs(p, x_cells), x_cells),
        in_specs=[vmem, vmem],
        out_specs=[vmem, vmem],
        out_shape=[
            jax.ShapeDtypeStruct(chunk, F32),
            jax.ShapeDtypeStruct((p.bands, 128), F32),
        ],
        scratch_shapes=[pltpu.VMEM((p.bands, LANES, share_y * p.both), F32)],
        name="rotate",
    )(everything, terms)
    landed = exchange(rotated.reshape((devices,) + chunk[2:]), AXES)

    def order(side, share):
        use, peer = divmod(share, peers)
        h, rest = divmod(peer, bc * ib)
        return ((h * bl + side) * copies + use) * bc * ib + rest

    keep_rows = (-(-p.side // p.group_y) + p.quarter // p.group_y) * chunk[2]
    filtered = pl.pallas_call(
        functools.partial(land_kernel, p, order),
        in_specs=[vmem] * 3,
        out_specs=vmem,
        out_shape=jax.ShapeDtypeStruct((2, band_block, x_cells, length * length), F32),
        scratch_shapes=[pltpu.VMEM((keep_rows, p.group_y * length), F32)],
        name="land",
    )(landed, jnp.asarray(tables["land_plus"]), jnp.asarray(tables["land_minus"]))

    table = table[:, 0]
    weights = jax.nn.sigmoid((fermi_level[0] - table) / TEMPER)
    band_energy = (jnp.sum(weights * table) / float(p.bands)).reshape(1)
    energies = lax.dynamic_slice_in_dim(table, lax.axis_index(BAND) * band_block, band_block, 0)
    return (filtered, energies, band_energy)


def solution(mesh):
    bands, slabs = mesh.shape["band"], mesh.shape["fft"]

    def body(start_bands, *rest):
        block = start_bands.shape[1] // bands
        sizes = (bands // 2, 2, 2, slabs // (4 * block), 2, block)
        fine = Mesh(mesh.devices.reshape(sizes), AXES)
        placed = (P(None, BAND, FFT, None), P(None, None, FFT), P(FFT, None), P(), P(), P())
        return jax.shard_map(
            functools.partial(local, sizes),
            mesh=fine,
            in_specs=placed,
            out_specs=(P(None, BAND, FFT, None), P(BAND), P()),
            check_vma=False,
        )(start_bands, *rest)

    return body
```
